512 devices in a mesh: row: 16 (over x_hi, y, core), col: 32 (over z, x_lo).
Axes of the slice: x: 4 (x_hi: 2, x_lo: 2; x = x_hi * 2 + x_lo), y: 4, z: 16, core: 2. Of those that a mesh axis runs over, the one named last changes fastest.
Arguments:
- volume: float32 [8, 4096, 4096], P(None, 'row', 'col'), may hold values from -6 to 6
- ray_weights: float32 [64, 4096], P(None, 'row'), may hold values from 0.5 to 2
- shear_weights: bfloat16 [64, 128, 128], replicated, may hold values from -0.5 to 0.5
- shear_offsets: int32 [64], replicated, may hold values from 0 to 31
- measured: float32 [64, 8, 4096], P('row', None, 'col'), may hold values from -6 to 6
Outputs:
- residual: float32 [64, 8, 4096], P('row', None, 'col')
- gradient: float32 [8, 4096, 4096], P(None, 'row', 'col')
The draws below stay inside these ranges and needn't reach their ends.
All inputs are finite; a program needn't handle non-finite values.
Results may differ from the reference program's by a relative error of at most 0.0003.
Values sent between devices are 32-bit elements; how exact they have to be, the bound alone decides.
No kernel may reach another device: no remote copies, remote signals or barrier semaphores. Data moves between devices by JAX's collectives and lax.ppermute only.
A program may use at most 64 MiB of HBM per device.

```python
import math
import jax
import jax.numpy as jnp
from jax import lax

CX = 256
CY = 128
SL = 8
NX = 4096
NY = 4096
ANGLES = 64
N_ROW = 16
N_COL = 32


def plant(values, key, smallest, high):
    extent = values.shape
    index_at = [jax.random.randint(jax.random.fold_in(key, axis), (), 0, extent[axis]) for axis in range(len(extent))]
    values = values.at[tuple(index_at)].set(smallest)
    longest = extent.index(max(extent))
    index_at[longest] = (index_at[longest] + 1) % extent[longest]
    return values.at[tuple(index_at)].set(high)


def steps_of(rng, dims, shards, smallest, high):
    factor_of, own = 1.0, jax.random.fold_in(rng, 6)
    for axis_at, parts in shards:
        heights = jnp.exp(jax.random.uniform(jax.random.fold_in(own, axis_at), (parts,), jnp.float32, smallest / len(shards), high / len(shards)))
        factor_of = factor_of * jnp.repeat(heights, dims[axis_at] // parts).reshape([-1 if axis == axis_at else 1 for axis in range(len(dims))])
    return factor_of


def noise(stream_key, dims, scale, bound, pieces=(), kind=jnp.bfloat16):
    array = scale * jax.random.normal(stream_key, dims, jnp.float32)
    if pieces:
        array = array * steps_of(stream_key, dims, pieces, -0.22, 0.18)
    return jnp.clip(array, -bound, bound).astype(kind)


def setup_inputs(seed: int = 0) -> dict:
    streams_of = jax.random.split(jax.random.key(seed), 6)
    volume = noise(streams_of[0], (SL, NX, NY), 1.0, 6.0, ((1, 16), (2, 32)), jnp.float32)
    ray_weights = jnp.clip(jnp.exp(math.log(2.0) - 1.3862944 * jax.random.uniform(streams_of[1], (ANGLES, NX), jnp.float32) ** steps_of(streams_of[1], (ANGLES, NX), ((1, 16),), -0.2, 0.2)), 0.5, 2.0)
    shear_weights = noise(streams_of[2], (ANGLES, CY, CY), CY ** -0.5, 0.5)
    shear_offsets = plant(jax.random.randint(streams_of[3], (ANGLES,), 0, N_COL), jax.random.fold_in(streams_of[3], 1), 0, N_COL - 1).astype(jnp.int32)
    measured = noise(streams_of[4], (ANGLES, SL, NY), 1.0, 6.0, ((0, 16), (2, 32)), jnp.float32)
    return dict(volume=volume, ray_weights=ray_weights, shear_weights=shear_weights, shear_offsets=shear_offsets, measured=measured)


def reference(volume, ray_weights, shear_weights, shear_offsets, measured):
    highest = lax.Precision.HIGHEST
    factor = 1.0 / math.sqrt(NX)
    blocks = volume.reshape(SL, N_ROW, CX, NY)
    weights_rows = ray_weights.reshape(ANGLES, N_ROW, CX)
    tilesum = jnp.einsum('arx,srxn->arsn', weights_rows, blocks, precision=highest) * factor
    shear = shear_weights.astype(jnp.float32)
    tiles = tilesum.reshape(ANGLES, N_ROW, SL, N_COL, CY)
    projected = jnp.einsum('arscy,ayz->arscz', tiles, shear, precision=highest)
    row_positions = jnp.arange(N_ROW, dtype=jnp.int32)
    col_positions = jnp.arange(N_COL, dtype=jnp.int32)
    moved = shear_offsets.astype(jnp.int32)[:, None, None] * row_positions[None, :, None]
    source = (col_positions[None, None, :] - moved) % N_COL
    full_shape = (ANGLES, N_ROW, SL, N_COL, CY)
    source_index = jnp.broadcast_to(source[:, :, None, :, None], full_shape).astype(jnp.int32)
    landed = jnp.take_along_axis(projected, source_index, axis=3)
    projection = lax.optimization_barrier(jnp.sum(landed, axis=1)).reshape(ANGLES, SL, NY)
    residual = projection - measured
    target = (col_positions[None, None, :] + moved) % N_COL
    target_index = jnp.broadcast_to(target[:, :, None, :, None], full_shape).astype(jnp.int32)
    resid_tiles = jnp.broadcast_to(residual.reshape(ANGLES, 1, SL, N_COL, CY), full_shape)
    pulled = jnp.take_along_axis(resid_tiles, target_index, axis=3)
    spread = jnp.einsum('arscz,ayz->arscy', pulled, shear, precision=highest)
    spread = spread.reshape(ANGLES, N_ROW, SL, NY)
    gradient = jnp.einsum('arx,arsn->srxn', weights_rows, spread, precision=highest) * factor
    return (residual, gradient.reshape(SL, NX, NY))
```

```python
import math

import jax
import jax.numpy as jnp
from jax import lax
from jax.experimental import pallas as pl
from jax.experimental.pallas import tpu as pltpu
from jax.sharding import PartitionSpec as P

VMEM = pl.BlockSpec(memory_space=pltpu.VMEM)
SMEM = pl.BlockSpec(memory_space=pltpu.SMEM)


def to_lines(rows, lines, tiles_ref, extra_ref, out_ref):
    for r in range(rows):
        out_ref[pl.ds(r, lines, stride=rows + 1), :] = tiles_ref[r * lines : (r + 1) * lines, :]
    out_ref[pl.ds(rows, lines, stride=rows + 1), :] = extra_ref[...]


def to_tiles(rows, lines, in_ref, tiles_ref, extra_ref):
    for r in range(rows):
        tiles_ref[r * lines : (r + 1) * lines, :] = in_ref[pl.ds(r, lines, stride=rows + 1), :]
    extra_ref[...] = in_ref[pl.ds(rows, lines, stride=rows + 1), :]


def halves(values):
    high = values.astype(jnp.bfloat16)
    low = (values - high.astype(jnp.float32)).astype(jnp.bfloat16)
    return jnp.concatenate([high, low], axis=0)


def middle(rows, cols, factor, offset_ref, in_ref, shear_ref, out_ref, sum_ref, twice_ref):
    offset = offset_ref[0]
    sum_ref[...] = jnp.zeros_like(sum_ref)
    for r in range(rows):
        at = lax.rem(offset * r, cols)
        window = pl.ds(at, cols)
        sum_ref[window, :] = sum_ref[window, :] + in_ref[pl.ds(r, cols, stride=rows + 1), :]
    total = (sum_ref[:cols, :] + sum_ref[cols:, :]) * factor
    shear = shear_ref[...]
    both = lax.dot_general(halves(total), shear, (((1,), (0,)), ((), ())), preferred_element_type=jnp.float32)
    residual = both[:cols] + both[cols:] - in_ref[pl.ds(rows, cols, stride=rows + 1), :]
    both = lax.dot_general(halves(residual), shear, (((1,), (1,)), ((), ())), preferred_element_type=jnp.float32)
    returning = both[:cols] + both[cols:]
    twice_ref[:cols, :] = returning
    twice_ref[cols:, :] = returning
    for r in range(rows):
        at = lax.rem(offset * r, cols)
        out_ref[pl.ds(r, cols, stride=rows + 1), :] = twice_ref[pl.ds(at, cols), :]
    out_ref[pl.ds(rows, cols, stride=rows + 1), :] = residual


def exchange(values, axis):
    rows, lanes = values.shape
    return lax.all_to_all(values.reshape(rows, 1, lanes), axis, 0, 0, tiled=True).reshape(rows, lanes)


def on_device(volume, ray_weights, shear_weights, shear_offsets, measured):
    highest = lax.Precision.HIGHEST
    rows = lax.axis_size("row")
    cols = lax.axis_size("col")
    slices, slab_rows, lanes = volume.shape
    angles = ray_weights.shape[0]
    per_owner = angles // rows
    lines = per_owner * slices
    factor = 1.0 / math.sqrt(slab_rows * rows)
    f32 = lambda count: jax.ShapeDtypeStruct((count, lanes), jnp.float32)
    angle = lax.axis_index("row") * per_owner + lax.axis_index("col") // slices
    shear = lax.dynamic_index_in_dim(shear_weights, angle, 0, keepdims=False)
    offset = lax.dynamic_slice_in_dim(shear_offsets, angle, 1, 0)

    tilesum = jnp.einsum("ax,sxy->asy", ray_weights, volume, precision=highest)
    received = exchange(tilesum.reshape(angles * slices, lanes), "row")
    packed = pl.pallas_call(
        lambda *refs: to_lines(rows, lines, *refs),
        out_shape=f32(lines * (rows + 1)),
        in_specs=[VMEM, VMEM],
        out_specs=VMEM,
        name="to_lines",
    )(received, measured.reshape(lines, lanes))
    line = exchange(packed, "col")
    answer = pl.pallas_call(
        lambda *refs: middle(rows, cols, factor, *refs),
        out_shape=f32(cols * (rows + 1)),
        in_specs=[SMEM, VMEM, VMEM],
        out_specs=VMEM,
        scratch_shapes=[pltpu.VMEM((2 * cols, lanes), jnp.float32), pltpu.VMEM((2 * cols, lanes), jnp.float32)],
        name="middle",
    )(offset, line, shear)
    returned = exchange(answer, "col")
    tiles, residual = pl.pallas_call(
        lambda *refs: to_tiles(rows, lines, *refs),
        out_shape=(f32(rows * lines), f32(lines)),
        in_specs=[VMEM],
        out_specs=(VMEM, VMEM),
        name="to_tiles",
    )(returned)
    arrived = exchange(tiles, "row").reshape(angles, slices, lanes)
    gradient = jnp.einsum("ax,asy->sxy", ray_weights, arrived, precision=highest) * factor
    return (residual.reshape(measured.shape), gradient)


def solution(mesh):
    placed = (P(None, "row", "col"), P(None, "row"), P(), P(), P("row", None, "col"))
    return jax.shard_map(
        on_device,
        mesh=mesh,
        in_specs=placed,
        out_specs=(P("row", None, "col"), P(None, "row", "col")),
        check_vma=False,
    )
```

```python
import math

import jax
import jax.numpy as jnp
from jax import lax
from jax.experimental import pallas as pl
from jax.experimental.pallas import tpu as pltpu
from jax.sharding import PartitionSpec as P

ANY = pl.BlockSpec(memory_space=pl.ANY)
VMEM = pl.BlockSpec(memory_space=pltpu.VMEM)
SMEM = pl.BlockSpec(memory_space=pltpu.SMEM)


def split(values):
    high = values.astype(jnp.bfloat16)
    return high, (values - high.astype(jnp.float32)).astype(jnp.bfloat16)


def dot(left, right, contract):
    return lax.dot_general(left, right, ((contract[:1], contract[1:]), ((), ())), preferred_element_type=jnp.float32)


def sums(volume_ref, weights_ref, shear_ref, tiles_ref, owned_ref, slab_ref, rays_ref, slab_sems, rays_sem, shear_sem, *, angle_of):
    slices, _, lanes = slab_ref.shape
    angles = rays_ref.shape[0]
    rays_copy = pltpu.make_async_copy(weights_ref, rays_ref, rays_sem)
    rays_copy.start()
    copies = [
        pltpu.make_async_copy(volume_ref.at[pl.ds(s, 2)], slab_ref.at[pl.ds(s, 2)], slab_sems.at[s // 2])
        for s in range(0, slices, 2)
    ]
    for copy in copies:
        copy.start()
    shear_copy = pltpu.make_async_copy(shear_ref.at[angle_of()], owned_ref, shear_sem)
    shear_copy.start()
    rays_copy.wait()
    rays_high, rays_low = split(rays_ref[...])
    rays_both = jnp.concatenate([rays_high, rays_low], axis=0)
    for s in range(0, slices, 2):
        copies[s // 2].wait()
        high, low = split(jnp.concatenate([slab_ref[s], slab_ref[s + 1]], axis=1))
        both = dot(rays_both, high, (1, 0))
        tiles = both[:angles] + both[angles:] + dot(rays_high, low, (1, 0))
        tiles_ref[pl.ds(s, angles, stride=slices), :] = tiles[:, :lanes]
        tiles_ref[pl.ds(s + 1, angles, stride=slices), :] = tiles[:, lanes:]
    shear_copy.wait()


def to_lines(tiles_ref, extra_ref, out_ref):
    lines = extra_ref.shape[0]
    rows = tiles_ref.shape[0] // lines
    for r in range(rows):
        out_ref[pl.ds(r, lines, stride=rows + 1), :] = tiles_ref[r * lines : (r + 1) * lines, :]
    out_ref[pl.ds(rows, lines, stride=rows + 1), :] = extra_ref[...]


def to_tiles(in_ref, tiles_ref, extra_ref):
    lines = extra_ref.shape[0]
    rows = tiles_ref.shape[0] // lines
    for r in range(rows):
        tiles_ref[r * lines : (r + 1) * lines, :] = in_ref[pl.ds(r, lines, stride=rows + 1), :]
    extra_ref[...] = in_ref[pl.ds(rows, lines, stride=rows + 1), :]


def middle(offset_ref, in_ref, shear_ref, out_ref, sum_ref, twice_ref, *, rows, cols, factor, angle_of):
    offset = offset_ref[angle_of()]
    sum_ref[...] = jnp.zeros_like(sum_ref)
    for r in range(rows):
        window = pl.ds(lax.rem(offset * r, cols), cols)
        sum_ref[window, :] = sum_ref[window, :] + in_ref[pl.ds(r, cols, stride=rows + 1), :]
    total = (sum_ref[:cols, :] + sum_ref[cols:, :]) * factor
    shear = shear_ref[...]
    both = dot(jnp.concatenate(split(total), axis=0), shear, (1, 0))
    residual = both[:cols] + both[cols:] - in_ref[pl.ds(rows, cols, stride=rows + 1), :]
    both = dot(jnp.concatenate(split(residual), axis=0), shear, (1, 1))
    returning = both[:cols] + both[cols:]
    twice_ref[:cols, :] = returning
    twice_ref[cols:, :] = returning
    for r in range(rows):
        out_ref[pl.ds(r, cols, stride=rows + 1), :] = twice_ref[pl.ds(lax.rem(offset * r, cols), cols), :]
    out_ref[pl.ds(rows, cols, stride=rows + 1), :] = residual


def spread_back(tiles_ref, rays_ref, residual_ref, out_ref, residual_out_ref, slab_ref, sems, residual_sem, *, factor):
    slices, _, lanes = slab_ref.shape
    angles = rays_ref.shape[0]
    residual_copy = pltpu.make_async_copy(residual_ref, residual_out_ref, residual_sem)
    residual_copy.start()
    rays = rays_ref[...] * factor
    high = rays.astype(jnp.bfloat16).astype(jnp.float32)
    rays = jnp.concatenate([high, high, rays - high], axis=0).T.astype(jnp.bfloat16)
    copies = []
    for s in range(0, slices, 2):
        pair = [tiles_ref[pl.ds(t, angles, stride=slices), :] for t in (s, s + 1)]
        high, low = split(jnp.concatenate(pair, axis=1))
        slab = dot(rays, jnp.concatenate([high, low, high], axis=0), (1, 0))
        slab_ref[s] = slab[:, :lanes]
        slab_ref[s + 1] = slab[:, lanes:]
        copy = pltpu.make_async_copy(slab_ref.at[pl.ds(s, 2)], out_ref.at[pl.ds(s, 2)], sems.at[s // 2])
        copy.start()
        copies.append(copy)
    for copy in copies:
        copy.wait()
    residual_copy.wait()


def exchange(values, axis):
    rows, lanes = values.shape
    return lax.all_to_all(values.reshape(rows, 1, lanes), axis, 0, 0, tiled=True).reshape(rows, lanes)


def near(values):
    return pltpu.with_memory_space_constraint(values, pltpu.VMEM)


def on_device(volume, ray_weights, shear_weights, shear_offsets, measured):
    rows = lax.axis_size("row")
    cols = lax.axis_size("col")
    slices, slab_rows, lanes = volume.shape
    angles = ray_weights.shape[0]
    per_owner = angles // rows
    lines = per_owner * slices
    factor = 1.0 / math.sqrt(slab_rows * rows)
    f32 = jnp.float32
    on_chip = lambda count: pltpu.VMEM((count, lanes), f32)
    angle_of = lambda: lax.axis_index("row") * per_owner + lax.axis_index("col") // slices

    tilesum, shear = pl.pallas_call(
        lambda *refs: sums(*refs, angle_of=angle_of),
        out_shape=(on_chip(angles * slices), pltpu.VMEM(shear_weights.shape[1:], shear_weights.dtype)),
        in_specs=[ANY, ANY, ANY],
        out_specs=(VMEM, VMEM),
        scratch_shapes=[
            pltpu.VMEM(volume.shape, f32),
            pltpu.VMEM(ray_weights.shape, f32),
            pltpu.SemaphoreType.DMA((slices // 2,)),
            pltpu.SemaphoreType.DMA,
            pltpu.SemaphoreType.DMA,
        ],
        name="sums",
    )(volume, ray_weights, shear_weights)
    received = exchange(tilesum, "row")
    packed = pl.pallas_call(
        to_lines,
        out_shape=on_chip(lines * (rows + 1)),
        in_specs=[VMEM, VMEM],
        out_specs=VMEM,
        name="to_lines",
    )(near(received), near(measured.reshape(lines, lanes)))
    line = exchange(packed, "col")
    answer = pl.pallas_call(
        lambda *refs: middle(*refs, rows=rows, cols=cols, factor=factor, angle_of=angle_of),
        out_shape=on_chip(cols * (rows + 1)),
        in_specs=[SMEM, VMEM, VMEM],
        out_specs=VMEM,
        scratch_shapes=[on_chip(2 * cols), on_chip(2 * cols)],
        name="middle",
    )(pltpu.with_memory_space_constraint(shear_offsets, pltpu.SMEM), near(line), near(shear))
    returned = exchange(answer, "col")
    tiles, residual = pl.pallas_call(
        to_tiles,
        out_shape=(on_chip(rows * lines), on_chip(lines)),
        in_specs=[VMEM],
        out_specs=(VMEM, VMEM),
        name="to_tiles",
    )(near(returned))
    arrived = exchange(tiles, "row")
    gradient, residual = pl.pallas_call(
        lambda *refs: spread_back(*refs, factor=factor),
        out_shape=(jax.ShapeDtypeStruct(volume.shape, f32), jax.ShapeDtypeStruct(residual.shape, f32)),
        in_specs=[VMEM, VMEM, VMEM],
        out_specs=(ANY, ANY),
        scratch_shapes=[
            pltpu.VMEM(volume.shape, f32),
            pltpu.SemaphoreType.DMA((slices // 2,)),
            pltpu.SemaphoreType.DMA,
        ],
        name="spread_back",
    )(near(arrived), near(ray_weights), near(residual))
    return (residual.reshape(measured.shape), gradient)


def solution(mesh):
    placed = (P(None, "row", "col"), P(None, "row"), P(), P(), P("row", None, "col"))
    return jax.shard_map(
        on_device,
        mesh=mesh,
        in_specs=placed,
        out_specs=(P("row", None, "col"), P(None, "row", "col")),
        check_vma=False,
    )
```

```python
import math

import jax
import jax.numpy as jnp
from jax import lax
from jax.experimental import pallas as pl
from jax.experimental.pallas import tpu as pltpu
from jax.sharding import PartitionSpec as P

ANY = pl.BlockSpec(memory_space=pl.ANY)
VMEM = pl.BlockSpec(memory_space=pltpu.VMEM)


def split(values):
    high = values.astype(jnp.bfloat16)
    return high, (values - high.astype(jnp.float32)).astype(jnp.bfloat16)


def dot(left, right, contract):
    return lax.dot_general(left, right, ((contract[:1], contract[1:]), ((), ())), preferred_element_type=jnp.float32)


def sums(volume_ref, weights_ref, shear_ref, offsets_ref, tiles_ref, owned_ref, offset_ref, slab_ref, rays_ref, table_ref, slab_sems, rays_sem, shear_sem, table_sem, *, angle_of):
    slices, _, lanes = slab_ref.shape
    angles = rays_ref.shape[0]
    half = slices // 2
    angle = angle_of()
    rays_copy = pltpu.make_async_copy(weights_ref, rays_ref, rays_sem)
    slab_copies = [
        pltpu.make_async_copy(volume_ref.at[pl.ds(s, half)], slab_ref.at[pl.ds(s, half)], slab_sems.at[s // half])
        for s in range(0, slices, half)
    ]
    shear_copy = pltpu.make_async_copy(shear_ref.at[angle], owned_ref, shear_sem)
    table_copy = pltpu.make_async_copy(offsets_ref, table_ref, table_sem)
    for copy in (rays_copy, *slab_copies, shear_copy, table_copy):
        copy.start()
    rays_copy.wait()
    rays_high, rays_low = split(rays_ref[...])
    rays_both = jnp.concatenate([rays_high, rays_low], axis=0)
    for s in range(0, slices, half):
        slab_copies[s // half].wait()
        high, low = split(jnp.concatenate([slab_ref[s + t] for t in range(half)], axis=1))
        both = dot(rays_both, high, (1, 0))
        tiles = both[:angles] + both[angles:] + dot(rays_high, low, (1, 0))
        for t in range(half):
            tiles_ref[pl.ds(s + t, angles, stride=slices), :] = tiles[:, t * lanes : (t + 1) * lanes]
    table_copy.wait()
    offset_ref[...] = jnp.full(offset_ref.shape, table_ref[angle], offset_ref.dtype)
    shear_copy.wait()


def to_lines(tiles_ref, extra_ref, out_ref):
    lines = extra_ref.shape[0]
    rows = tiles_ref.shape[0] // lines
    for r in range(rows):
        out_ref[pl.ds(r, lines, stride=rows + 1), :] = tiles_ref[r * lines : (r + 1) * lines, :]
    out_ref[pl.ds(rows, lines, stride=rows + 1), :] = extra_ref[...]


def to_tiles(in_ref, tiles_ref, extra_ref):
    lines = extra_ref.shape[0]
    rows = tiles_ref.shape[0] // lines
    for r in range(rows):
        tiles_ref[r * lines : (r + 1) * lines, :] = in_ref[pl.ds(r, lines, stride=rows + 1), :]
    extra_ref[...] = in_ref[pl.ds(rows, lines, stride=rows + 1), :]


def middle(offset_ref, in_ref, shear_ref, out_ref, sum_ref, twice_ref, *, rows, cols, factor):
    offset = offset_ref[0, 0]
    sum_ref[...] = jnp.zeros_like(sum_ref)
    for r in range(rows):
        window = pl.ds(lax.rem(offset * r, cols), cols)
        sum_ref[window, :] = sum_ref[window, :] + in_ref[pl.ds(r, cols, stride=rows + 1), :]
    total = (sum_ref[:cols, :] + sum_ref[cols:, :]) * factor
    shear = shear_ref[...]
    both = dot(jnp.concatenate(split(total), axis=0), shear, (1, 0))
    residual = both[:cols] + both[cols:] - in_ref[pl.ds(rows, cols, stride=rows + 1), :]
    both = dot(jnp.concatenate(split(residual), axis=0), shear, (1, 1))
    returning = both[:cols] + both[cols:]
    twice_ref[:cols, :] = returning
    twice_ref[cols:, :] = returning
    for r in range(rows):
        out_ref[pl.ds(r, cols, stride=rows + 1), :] = twice_ref[pl.ds(lax.rem(offset * r, cols), cols), :]
    out_ref[pl.ds(rows, cols, stride=rows + 1), :] = residual


def spread_back(tiles_ref, rays_ref, residual_ref, out_ref, residual_out_ref, slab_ref, sems, residual_sem, *, factor):
    slices, _, lanes = slab_ref.shape
    angles = rays_ref.shape[0]
    residual_copy = pltpu.make_async_copy(residual_ref, residual_out_ref, residual_sem)
    residual_copy.start()
    rays = rays_ref[...] * factor
    high = rays.astype(jnp.bfloat16).astype(jnp.float32)
    rays = jnp.concatenate([high, high, rays - high], axis=0).T.astype(jnp.bfloat16)
    copies = []
    for s in range(0, slices, 2):
        pair = [tiles_ref[pl.ds(t, angles, stride=slices), :] for t in (s, s + 1)]
        high, low = split(jnp.concatenate(pair, axis=1))
        slab = dot(rays, jnp.concatenate([high, low, high], axis=0), (1, 0))
        slab_ref[s] = slab[:, :lanes]
        slab_ref[s + 1] = slab[:, lanes:]
        copy = pltpu.make_async_copy(slab_ref.at[pl.ds(s, 2)], out_ref.at[pl.ds(s, 2)], sems.at[s // 2])
        copy.start()
        copies.append(copy)
    for copy in copies:
        copy.wait()
    residual_copy.wait()


def exchange(values, axis):
    rows, lanes = values.shape
    return lax.all_to_all(values.reshape(rows, 1, lanes), axis, 0, 0, tiled=True).reshape(rows, lanes)


def near(values):
    return pltpu.with_memory_space_constraint(values, pltpu.VMEM)


def on_device(volume, ray_weights, shear_weights, shear_offsets, measured):
    rows = lax.axis_size("row")
    cols = lax.axis_size("col")
    slices, slab_rows, lanes = volume.shape
    angles = ray_weights.shape[0]
    per_owner = angles // rows
    lines = per_owner * slices
    factor = 1.0 / math.sqrt(slab_rows * rows)
    f32 = jnp.float32
    on_chip = lambda count: pltpu.VMEM((count, lanes), f32)
    angle_of = lambda: lax.axis_index("row") * per_owner + lax.axis_index("col") // slices

    tilesum, shear, offset = pl.pallas_call(
        lambda *refs: sums(*refs, angle_of=angle_of),
        out_shape=(
            on_chip(angles * slices),
            pltpu.VMEM(shear_weights.shape[1:], shear_weights.dtype),
            pltpu.VMEM((8, lanes), shear_offsets.dtype),
        ),
        in_specs=[ANY, ANY, ANY, ANY],
        out_specs=(VMEM, VMEM, VMEM),
        scratch_shapes=[
            pltpu.VMEM(volume.shape, f32),
            pltpu.VMEM(ray_weights.shape, f32),
            pltpu.SMEM(shear_offsets.shape, shear_offsets.dtype),
            pltpu.SemaphoreType.DMA((2,)),
            pltpu.SemaphoreType.DMA,
            pltpu.SemaphoreType.DMA,
            pltpu.SemaphoreType.DMA,
        ],
        name="sums",
    )(volume, ray_weights, shear_weights, shear_offsets)
    received = exchange(tilesum, "row")
    packed = pl.pallas_call(
        to_lines,
        out_shape=on_chip(lines * (rows + 1)),
        in_specs=[VMEM, VMEM],
        out_specs=VMEM,
        name="to_lines",
    )(near(received), near(measured.reshape(lines, lanes)))
    line = exchange(packed, "col")
    answer = pl.pallas_call(
        lambda *refs: middle(*refs, rows=rows, cols=cols, factor=factor),
        out_shape=on_chip(cols * (rows + 1)),
        in_specs=[VMEM, VMEM, VMEM],
        out_specs=VMEM,
        scratch_shapes=[on_chip(2 * cols), on_chip(2 * cols)],
        name="middle",
    )(near(offset), near(line), near(shear))
    returned = exchange(answer, "col")
    tiles, residual = pl.pallas_call(
        to_tiles,
        out_shape=(on_chip(rows * lines), on_chip(lines)),
        in_specs=[VMEM],
        out_specs=(VMEM, VMEM),
        name="to_tiles",
    )(near(returned))
    arrived = exchange(tiles, "row")
    gradient, residual = pl.pallas_call(
        lambda *refs: spread_back(*refs, factor=factor),
        out_shape=(jax.ShapeDtypeStruct(volume.shape, f32), jax.ShapeDtypeStruct(residual.shape, f32)),
        in_specs=[VMEM, VMEM, VMEM],
        out_specs=(ANY, ANY),
        scratch_shapes=[
            pltpu.VMEM(volume.shape, f32),
            pltpu.SemaphoreType.DMA((slices // 2,)),
            pltpu.SemaphoreType.DMA,
        ],
        name="spread_back",
    )(near(arrived), near(ray_weights), near(residual))
    return (residual.reshape(measured.shape), gradient)


def solution(mesh):
    placed = (P(None, "row", "col"), P(None, "row"), P(), P(), P("row", None, "col"))
    return jax.shard_map(
        on_device,
        mesh=mesh,
        in_specs=placed,
        out_specs=(P("row", None, "col"), P(None, "row", "col")),
        check_vma=False,
    )
```

```python
import math

import jax
import jax.numpy as jnp
from jax import lax
from jax.experimental import pallas as pl
from jax.experimental.pallas import tpu as pltpu
from jax.sharding import Mesh, PartitionSpec as P

NEAR = 4
ANY = pl.BlockSpec(memory_space=pl.ANY)
VMEM = pl.BlockSpec(memory_space=pltpu.VMEM)


def split(values):
    high = values.astype(jnp.bfloat16)
    return high, (values - high.astype(jnp.float32)).astype(jnp.bfloat16)


def dot(left, right, contract):
    return lax.dot_general(left, right, ((contract[:1], contract[1:]), ((), ())), preferred_element_type=jnp.float32)


def sums(volume_ref, weights_ref, shear_ref, offsets_ref, tiles_ref, owned_ref, offset_ref, slab_ref, rays_ref, table_ref, slab_sems, rays_sem, shear_sem, table_sem, *, row_of, angle_of):
    slices, _, lanes = slab_ref.shape
    angles = rays_ref.shape[0]
    owned = owned_ref.shape[0]
    half = slices // 2
    rays_copy = pltpu.make_async_copy(weights_ref, rays_ref, rays_sem)
    slab_copies = [
        pltpu.make_async_copy(volume_ref.at[pl.ds(s, half)], slab_ref.at[pl.ds(s, half)], slab_sems.at[s // half])
        for s in range(0, slices, half)
    ]
    shear_copy = pltpu.make_async_copy(shear_ref.at[pl.ds(row_of() * owned, owned)], owned_ref, shear_sem)
    table_copy = pltpu.make_async_copy(offsets_ref, table_ref, table_sem)
    for copy in (rays_copy, *slab_copies, shear_copy, table_copy):
        copy.start()
    rays_copy.wait()
    rays_high, rays_low = split(rays_ref[...])
    rays_both = jnp.concatenate([rays_high, rays_low], axis=0)
    for s in range(0, slices, half):
        slab_copies[s // half].wait()
        high, low = split(jnp.concatenate([slab_ref[s + t] for t in range(half)], axis=1))
        both = dot(rays_both, high, (1, 0))
        tiles = both[:angles] + both[angles:] + dot(rays_high, low, (1, 0))
        for t in range(half):
            tiles_ref[pl.ds(s + t, angles, stride=slices), :] = tiles[:, t * lanes : (t + 1) * lanes]
    table_copy.wait()
    offset_ref[...] = jnp.full(offset_ref.shape, table_ref[angle_of()], offset_ref.dtype)
    shear_copy.wait()


def push(offset_ref, tiles_ref, line_ref, *, first_of):
    cols = line_ref.shape[0]
    offset = offset_ref[0, 0]
    first = first_of()
    line_ref[...] = jnp.zeros_like(line_ref)
    for t in range(tiles_ref.shape[0]):
        at = lax.rem(first + t % NEAR + offset * (t // NEAR), cols)
        line_ref[at] = line_ref[at] + tiles_ref[t]


def pull(offset_ref, line_ref, tiles_ref, *, first_of):
    cols = line_ref.shape[0]
    offset = offset_ref[0, 0]
    first = first_of()
    for t in range(tiles_ref.shape[0]):
        tiles_ref[t] = line_ref[lax.rem(first + t % NEAR + offset * (t // NEAR), cols)]


def middle(parts_ref, shear_ref, measured_ref, copies_ref, residual_ref, *, factor):
    count, slices, _ = parts_ref.shape
    for j in range(NEAR):
        total = parts_ref[j]
        for t in range(j + NEAR, count, NEAR):
            total = total + parts_ref[t]
        shear = shear_ref[j]
        both = dot(jnp.concatenate(split(total * factor), axis=0), shear, (1, 0))
        residual = both[:slices] + both[slices:] - measured_ref[j]
        residual_ref[j] = residual
        both = dot(jnp.concatenate(split(residual), axis=0), shear, (1, 1))
        returning = both[:slices] + both[slices:]
        for t in range(j, count, NEAR):
            copies_ref[t] = returning


def spread_back(tiles_ref, rays_ref, residual_ref, out_ref, residual_out_ref, slab_ref, sems, residual_sem, *, factor):
    slices, _, lanes = slab_ref.shape
    angles = rays_ref.shape[0]
    residual_copy = pltpu.make_async_copy(residual_ref, residual_out_ref, residual_sem)
    residual_copy.start()
    rays = rays_ref[...] * factor
    high = rays.astype(jnp.bfloat16).astype(jnp.float32)
    rays = jnp.concatenate([high, high, rays - high], axis=0).T.astype(jnp.bfloat16)
    copies = []
    for s in range(0, slices, 2):
        pair = [tiles_ref[pl.ds(t, angles, stride=slices), :] for t in (s, s + 1)]
        high, low = split(jnp.concatenate(pair, axis=1))
        slab = dot(rays, jnp.concatenate([high, low, high], axis=0), (1, 0))
        slab_ref[s] = slab[:, :lanes]
        slab_ref[s + 1] = slab[:, lanes:]
        copy = pltpu.make_async_copy(slab_ref.at[pl.ds(s, 2)], out_ref.at[pl.ds(s, 2)], sems.at[s // 2])
        copy.start()
        copies.append(copy)
    for copy in copies:
        copy.wait()
    residual_copy.wait()


def exchange(values, axes):
    return lax.all_to_all(values, axes, 0, 0, tiled=True)


def near(values):
    return pltpu.with_memory_space_constraint(values, pltpu.VMEM)


def on_device(volume, ray_weights, shear_weights, shear_offsets, measured):
    rows = lax.axis_size("row")
    cols = lax.axis_size(("far", "near"))
    slices, slab_rows, lanes = volume.shape
    angles = ray_weights.shape[0]
    factor = 1.0 / math.sqrt(slab_rows * rows)
    f32 = jnp.float32
    tiles_of = lambda count: pltpu.VMEM((count, slices, lanes), f32)
    row_of = lambda: lax.axis_index("row")
    angle_of = lambda: lax.axis_index("row") * NEAR + lax.axis_index("near")
    first_of = lambda: lax.axis_index("far") * NEAR

    tilesum, shear, offset = pl.pallas_call(
        lambda *refs: sums(*refs, row_of=row_of, angle_of=angle_of),
        out_shape=(
            pltpu.VMEM((angles * slices, lanes), f32),
            pltpu.VMEM((NEAR,) + shear_weights.shape[1:], shear_weights.dtype),
            pltpu.VMEM((8, lanes), shear_offsets.dtype),
        ),
        in_specs=[ANY, ANY, ANY, ANY],
        out_specs=(VMEM, VMEM, VMEM),
        scratch_shapes=[
            pltpu.VMEM(volume.shape, f32),
            pltpu.VMEM(ray_weights.shape, f32),
            pltpu.SMEM(shear_offsets.shape, shear_offsets.dtype),
            pltpu.SemaphoreType.DMA((2,)),
            pltpu.SemaphoreType.DMA,
            pltpu.SemaphoreType.DMA,
            pltpu.SemaphoreType.DMA,
        ],
        name="sums",
    )(volume, ray_weights, shear_weights, shear_offsets)
    received = exchange(tilesum.reshape(angles, slices, lanes), ("row", "near"))
    line = pl.pallas_call(
        lambda *refs: push(*refs, first_of=first_of),
        out_shape=tiles_of(cols),
        in_specs=[VMEM, VMEM],
        out_specs=VMEM,
        name="push",
    )(near(offset), near(received))
    parts = exchange(line, ("far", "near"))
    answer, residual = pl.pallas_call(
        lambda *refs: middle(*refs, factor=factor),
        out_shape=(tiles_of(cols), tiles_of(NEAR)),
        in_specs=[VMEM, VMEM, VMEM],
        out_specs=(VMEM, VMEM),
        name="middle",
    )(near(parts), near(shear), near(measured))
    returned = exchange(answer, ("far", "near"))
    tiles = pl.pallas_call(
        lambda *refs: pull(*refs, first_of=first_of),
        out_shape=tiles_of(angles),
        in_specs=[VMEM, VMEM],
        out_specs=VMEM,
        name="pull",
    )(near(offset), near(returned))
    arrived = exchange(tiles, ("row", "near")).reshape(angles * slices, lanes)
    gradient, residual = pl.pallas_call(
        lambda *refs: spread_back(*refs, factor=factor),
        out_shape=(jax.ShapeDtypeStruct(volume.shape, f32), jax.ShapeDtypeStruct(residual.shape, f32)),
        in_specs=[VMEM, VMEM, VMEM],
        out_specs=(ANY, ANY),
        scratch_shapes=[
            pltpu.VMEM(volume.shape, f32),
            pltpu.SemaphoreType.DMA((slices // 2,)),
            pltpu.SemaphoreType.DMA,
        ],
        name="spread_back",
    )(near(arrived), near(ray_weights), near(residual))
    return (residual, gradient)


def solution(mesh):
    rows, cols = mesh.devices.shape
    cut = Mesh(mesh.devices.reshape(rows, cols // NEAR, NEAR), ("row", "far", "near"))
    columns = ("far", "near")
    placed = (P(None, "row", columns), P(None, "row"), P(), P(), P("row", None, columns))
    return jax.shard_map(
        on_device,
        mesh=cut,
        in_specs=placed,
        out_specs=(P("row", None, columns), P(None, "row", columns)),
        check_vma=False,
    )
```

```python
import math

import jax
import jax.numpy as jnp
from jax import lax
from jax.experimental import pallas as pl
from jax.experimental.pallas import tpu as pltpu
from jax.sharding import Mesh, PartitionSpec as P

NEAR = 4
ANY = pl.BlockSpec(memory_space=pl.ANY)
VMEM = pl.BlockSpec(memory_space=pltpu.VMEM)


def split(values):
    high = values.astype(jnp.bfloat16)
    return high, (values - high.astype(jnp.float32)).astype(jnp.bfloat16)


def dot(left, right, contract):
    return lax.dot_general(left, right, ((contract[:1], contract[1:]), ((), ())), preferred_element_type=jnp.float32)


def sums(volume_ref, weights_ref, shear_ref, offsets_ref, tiles_ref, owned_ref, offset_ref, across_ref, slab_ref, rays_ref, table_ref, slab_sems, rays_sem, shear_sem, table_sem, *, row_of, angle_of, factor):
    slices, _, lanes = slab_ref.shape
    angles = rays_ref.shape[0]
    owned = owned_ref.shape[0]
    half = slices // 2
    rays_copy = pltpu.make_async_copy(weights_ref, rays_ref, rays_sem)
    slab_copies = [
        pltpu.make_async_copy(volume_ref.at[pl.ds(s, half)], slab_ref.at[pl.ds(s, half)], slab_sems.at[s // half])
        for s in range(0, slices, half)
    ]
    shear_copy = pltpu.make_async_copy(shear_ref.at[pl.ds(row_of() * owned, owned)], owned_ref, shear_sem)
    table_copy = pltpu.make_async_copy(offsets_ref, table_ref, table_sem)
    for copy in (rays_copy, *slab_copies, shear_copy, table_copy):
        copy.start()
    rays_copy.wait()
    rays_high, rays_low = split(rays_ref[...])
    rays_both = jnp.concatenate([rays_high, rays_low], axis=0)
    scaled = rays_ref[...] * factor
    high = scaled.astype(jnp.bfloat16).astype(jnp.float32)
    across_ref[...] = jnp.concatenate([high, high, scaled - high], axis=0).T.astype(jnp.bfloat16)
    for s in range(0, slices, half):
        slab_copies[s // half].wait()
        high, low = split(jnp.concatenate([slab_ref[s + t] for t in range(half)], axis=1))
        both = dot(rays_both, high, (1, 0))
        tiles = both[:angles] + both[angles:] + dot(rays_high, low, (1, 0))
        for t in range(half):
            tiles_ref[pl.ds(s + t, angles, stride=slices), :] = tiles[:, t * lanes : (t + 1) * lanes]
    table_copy.wait()
    offset_ref[...] = jnp.full(offset_ref.shape, table_ref[angle_of()], offset_ref.dtype)
    shear_copy.wait()


def push(offset_ref, tiles_ref, line_ref, sum_ref, *, first_of):
    cols = line_ref.shape[0]
    rows = tiles_ref.shape[0] // NEAR
    room = sum_ref.shape[0] // 2
    offset = offset_ref[0, 0]
    first = first_of()
    sum_ref[...] = jnp.zeros_like(sum_ref)
    for r in range(rows):
        window = pl.ds(lax.rem(first + offset * r, cols) + r % 2 * room, NEAR)
        sum_ref[window] = sum_ref[window] + tiles_ref[r * NEAR : (r + 1) * NEAR]
    line_ref[...] = sum_ref[:cols] + sum_ref[room : room + cols]
    line_ref[: room - cols] = line_ref[: room - cols] + (sum_ref[cols:room] + sum_ref[room + cols :])


def pull(offset_ref, line_ref, tiles_ref, twice_ref, *, first_of):
    cols = line_ref.shape[0]
    rows = tiles_ref.shape[0] // NEAR
    offset = offset_ref[0, 0]
    first = first_of()
    twice_ref[:cols] = line_ref[...]
    twice_ref[cols:] = line_ref[:NEAR]
    for r in range(rows):
        tiles_ref[r * NEAR : (r + 1) * NEAR] = twice_ref[pl.ds(lax.rem(first + offset * r, cols), NEAR)]


def middle(parts_ref, shear_ref, measured_ref, copies_ref, residual_ref, *, factor):
    count, slices, _ = parts_ref.shape
    residuals = []
    for j in range(NEAR):
        shares = [parts_ref[t] for t in range(j, count, NEAR)]
        while len(shares) > 1:
            shares = [sum(shares[t : t + 2]) for t in range(0, len(shares), 2)]
        both = dot(jnp.concatenate(split(shares[0] * factor), axis=0), shear_ref[j], (1, 0))
        residuals.append(both[:slices] + both[slices:] - measured_ref[j])
    for j in range(NEAR):
        residual_ref[j] = residuals[j]
        both = dot(jnp.concatenate(split(residuals[j]), axis=0), shear_ref[j], (1, 1))
        returning = both[:slices] + both[slices:]
        for t in range(j, count, NEAR):
            copies_ref[t] = returning


def spread_back(tiles_ref, across_ref, residual_ref, out_ref, residual_out_ref, slab_ref, sems, residual_sem):
    slices, _, lanes = slab_ref.shape
    angles = tiles_ref.shape[0] // slices
    residual_copy = pltpu.make_async_copy(residual_ref, residual_out_ref, residual_sem)
    residual_copy.start()
    across = across_ref[...]
    copies = []
    for s in range(0, slices, 2):
        pair = [tiles_ref[pl.ds(t, angles, stride=slices), :] for t in (s, s + 1)]
        high, low = split(jnp.concatenate(pair, axis=1))
        slab = dot(across, jnp.concatenate([high, low, high], axis=0), (1, 0))
        slab_ref[s] = slab[:, :lanes]
        slab_ref[s + 1] = slab[:, lanes:]
        copy = pltpu.make_async_copy(slab_ref.at[pl.ds(s, 2)], out_ref.at[pl.ds(s, 2)], sems.at[s // 2])
        copy.start()
        copies.append(copy)
    for copy in copies:
        copy.wait()
    residual_copy.wait()


def exchange(values, axes):
    return lax.all_to_all(values, axes, 0, 0, tiled=True)


def near(values):
    return pltpu.with_memory_space_constraint(values, pltpu.VMEM)


def on_device(volume, ray_weights, shear_weights, shear_offsets, measured):
    rows = lax.axis_size("row")
    cols = lax.axis_size(("far", "near"))
    slices, slab_rows, lanes = volume.shape
    angles = ray_weights.shape[0]
    factor = 1.0 / math.sqrt(slab_rows * rows)
    f32 = jnp.float32
    tiles_of = lambda count: pltpu.VMEM((count, slices, lanes), f32)
    row_of = lambda: lax.axis_index("row")
    angle_of = lambda: lax.axis_index("row") * NEAR + lax.axis_index("near")
    first_of = lambda: lax.axis_index("far") * NEAR

    tilesum, shear, offset, across = pl.pallas_call(
        lambda *refs: sums(*refs, row_of=row_of, angle_of=angle_of, factor=factor),
        out_shape=(
            pltpu.VMEM((angles * slices, lanes), f32),
            pltpu.VMEM((NEAR,) + shear_weights.shape[1:], shear_weights.dtype),
            pltpu.VMEM((8, lanes), shear_offsets.dtype),
            pltpu.VMEM((slab_rows, 3 * angles), jnp.bfloat16),
        ),
        in_specs=[ANY, ANY, ANY, ANY],
        out_specs=(VMEM, VMEM, VMEM, VMEM),
        scratch_shapes=[
            pltpu.VMEM(volume.shape, f32),
            pltpu.VMEM(ray_weights.shape, f32),
            pltpu.SMEM(shear_offsets.shape, shear_offsets.dtype),
            pltpu.SemaphoreType.DMA((2,)),
            pltpu.SemaphoreType.DMA,
            pltpu.SemaphoreType.DMA,
            pltpu.SemaphoreType.DMA,
        ],
        name="sums",
    )(volume, ray_weights, shear_weights, shear_offsets)
    received = exchange(tilesum.reshape(angles, slices, lanes), ("row", "near"))
    line = pl.pallas_call(
        lambda *refs: push(*refs, first_of=first_of),
        out_shape=tiles_of(cols),
        in_specs=[VMEM, VMEM],
        out_specs=VMEM,
        scratch_shapes=[tiles_of(2 * (cols + NEAR))],
        name="push",
    )(near(offset), near(received))
    parts = exchange(line, ("far", "near"))
    answer, residual = pl.pallas_call(
        lambda *refs: middle(*refs, factor=factor),
        out_shape=(tiles_of(cols), tiles_of(NEAR)),
        in_specs=[VMEM, VMEM, VMEM],
        out_specs=(VMEM, VMEM),
        name="middle",
    )(near(parts), near(shear), near(measured))
    returned = exchange(answer, ("far", "near"))
    tiles = pl.pallas_call(
        lambda *refs: pull(*refs, first_of=first_of),
        out_shape=tiles_of(angles),
        in_specs=[VMEM, VMEM],
        out_specs=VMEM,
        scratch_shapes=[tiles_of(cols + NEAR)],
        name="pull",
    )(near(offset), near(returned))
    arrived = exchange(tiles, ("row", "near")).reshape(angles * slices, lanes)
    gradient, residual = pl.pallas_call(
        spread_back,
        out_shape=(jax.ShapeDtypeStruct(volume.shape, f32), jax.ShapeDtypeStruct(residual.shape, f32)),
        in_specs=[VMEM, VMEM, VMEM],
        out_specs=(ANY, ANY),
        scratch_shapes=[
            pltpu.VMEM(volume.shape, f32),
            pltpu.SemaphoreType.DMA((slices // 2,)),
            pltpu.SemaphoreType.DMA,
        ],
        name="spread_back",
    )(near(arrived), near(across), near(residual))
    return (residual, gradient)


def solution(mesh):
    rows, cols = mesh.devices.shape
    cut = Mesh(mesh.devices.reshape(rows, cols // NEAR, NEAR), ("row", "far", "near"))
    columns = ("far", "near")
    placed = (P(None, "row", columns), P(None, "row"), P(), P(), P("row", None, columns))
    return jax.shard_map(
        on_device,
        mesh=cut,
        in_specs=placed,
        out_specs=(P("row", None, columns), P(None, "row", columns)),
        check_vma=False,
    )
```

```python
import math

import jax
import jax.numpy as jnp
from jax import lax
from jax.experimental import pallas as pl
from jax.experimental.pallas import tpu as pltpu
from jax.sharding import Mesh, PartitionSpec as P

NEAR = 4
ANY = pl.BlockSpec(memory_space=pl.ANY)
VMEM = pl.BlockSpec(memory_space=pltpu.VMEM)


def row_order(rows):
    return sorted(range(rows), key=lambda r: (r % 2 == 0, -r))


def split(values):
    high = values.astype(jnp.bfloat16)
    return high, (values - high.astype(jnp.float32)).astype(jnp.bfloat16)


def dot(left, right, contract):
    return lax.dot_general(left, right, ((contract[:1], contract[1:]), ((), ())), preferred_element_type=jnp.float32)


def sums(volume_ref, weights_ref, shear_ref, offsets_ref, tiles_ref, owned_ref, offset_ref, across_ref, slab_ref, rays_ref, sorted_ref, table_ref, slab_sems, rays_sem, shear_sem, table_sem, *, row_of, angle_of, factor):
    slices, _, lanes = slab_ref.shape
    angles = rays_ref.shape[0]
    owned = owned_ref.shape[0]
    half = slices // 2
    rays_copy = pltpu.make_async_copy(weights_ref, rays_ref, rays_sem)
    slab_copies = [
        pltpu.make_async_copy(volume_ref.at[pl.ds(s, half)], slab_ref.at[pl.ds(s, half)], slab_sems.at[s // half])
        for s in range(0, slices, half)
    ]
    shear_copy = pltpu.make_async_copy(shear_ref.at[pl.ds(row_of() * owned, owned)], owned_ref, shear_sem)
    table_copy = pltpu.make_async_copy(offsets_ref, table_ref, table_sem)
    for copy in (rays_copy, *slab_copies, shear_copy, table_copy):
        copy.start()
    rays_copy.wait()
    for i, r in enumerate(row_order(angles // NEAR)):
        sorted_ref[i * NEAR : (i + 1) * NEAR, :] = rays_ref[r * NEAR : (r + 1) * NEAR, :]
    rays = sorted_ref[...]
    rays_high, rays_low = split(rays)
    rays_both = jnp.concatenate([rays_high, rays_low], axis=0)
    scaled = rays * factor
    high = scaled.astype(jnp.bfloat16).astype(jnp.float32)
    across_ref[...] = jnp.concatenate([high, high, scaled - high], axis=0).T.astype(jnp.bfloat16)
    for s in range(0, slices, half):
        slab_copies[s // half].wait()
        high, low = split(jnp.concatenate([slab_ref[s + t] for t in range(half)], axis=1))
        both = dot(rays_both, high, (1, 0))
        tiles = both[:angles] + both[angles:] + dot(rays_high, low, (1, 0))
        for t in range(half):
            tiles_ref[pl.ds(s + t, angles, stride=slices), :] = tiles[:, t * lanes : (t + 1) * lanes]
    table_copy.wait()
    offset_ref[...] = jnp.full(offset_ref.shape, table_ref[angle_of()], offset_ref.dtype)
    shear_copy.wait()


def push(offset_ref, tiles_ref, line_ref, sum_ref, *, first_of):
    cols = line_ref.shape[0]
    rows = tiles_ref.shape[0] // NEAR
    room = sum_ref.shape[0] // 2
    offset = offset_ref[0, 0]
    first = first_of()
    sum_ref[...] = jnp.zeros_like(sum_ref)
    for i, r in enumerate(row_order(rows)):
        window = pl.ds(lax.rem(first + offset * r, cols) + i % 2 * room, NEAR)
        sum_ref[window] = sum_ref[window] + tiles_ref[i * NEAR : (i + 1) * NEAR]
    line_ref[...] = sum_ref[:cols] + sum_ref[room : room + cols]
    line_ref[: room - cols] = line_ref[: room - cols] + (sum_ref[cols:room] + sum_ref[room + cols :])


def pull(offset_ref, line_ref, tiles_ref, twice_ref, *, first_of):
    cols = line_ref.shape[0]
    rows = tiles_ref.shape[0] // NEAR
    offset = offset_ref[0, 0]
    first = first_of()
    twice_ref[:cols] = line_ref[...]
    twice_ref[cols:] = line_ref[:NEAR]
    for i, r in enumerate(row_order(rows)):
        tiles_ref[i * NEAR : (i + 1) * NEAR] = twice_ref[pl.ds(lax.rem(first + offset * r, cols), NEAR)]


def middle(parts_ref, shear_ref, measured_ref, copies_ref, residual_ref, *, factor):
    count, slices, _ = parts_ref.shape
    residuals = []
    for j in range(NEAR):
        shares = [parts_ref[t] for t in range(j, count, NEAR)]
        while len(shares) > 1:
            shares = [sum(shares[t : t + 2]) for t in range(0, len(shares), 2)]
        both = dot(jnp.concatenate(split(shares[0] * factor), axis=0), shear_ref[j], (1, 0))
        residuals.append(both[:slices] + both[slices:] - measured_ref[j])
    for j in range(NEAR):
        residual_ref[j] = residuals[j]
        both = dot(jnp.concatenate(split(residuals[j]), axis=0), shear_ref[j], (1, 1))
        returning = both[:slices] + both[slices:]
        for t in range(j, count, NEAR):
            copies_ref[t] = returning


def spread_back(tiles_ref, across_ref, residual_ref, out_ref, residual_out_ref, slab_ref, sems, residual_sem):
    slices, _, lanes = slab_ref.shape
    angles = tiles_ref.shape[0] // slices
    residual_copy = pltpu.make_async_copy(residual_ref, residual_out_ref, residual_sem)
    residual_copy.start()
    across = across_ref[...]
    copies = []
    for s in range(0, slices, 2):
        pair = [tiles_ref[pl.ds(t, angles, stride=slices), :] for t in (s, s + 1)]
        high, low = split(jnp.concatenate(pair, axis=1))
        slab = dot(across, jnp.concatenate([high, low, high], axis=0), (1, 0))
        slab_ref[s] = slab[:, :lanes]
        slab_ref[s + 1] = slab[:, lanes:]
        copy = pltpu.make_async_copy(slab_ref.at[pl.ds(s, 2)], out_ref.at[pl.ds(s, 2)], sems.at[s // 2])
        copy.start()
        copies.append(copy)
    for copy in copies:
        copy.wait()
    residual_copy.wait()


def exchange(values, axes, groups=None):
    return lax.all_to_all(values, axes, 0, 0, tiled=True, axis_index_groups=groups)


def near(values):
    return pltpu.with_memory_space_constraint(values, pltpu.VMEM)


def on_device(volume, ray_weights, shear_weights, shear_offsets, measured):
    rows = lax.axis_size("row")
    cols = lax.axis_size(("far", "near"))
    slices, slab_rows, lanes = volume.shape
    angles = ray_weights.shape[0]
    factor = 1.0 / math.sqrt(slab_rows * rows)
    f32 = jnp.float32
    peers = [[r * NEAR + k for r in row_order(rows) for k in range(NEAR)]]
    tiles_of = lambda count: pltpu.VMEM((count, slices, lanes), f32)
    row_of = lambda: lax.axis_index("row")
    angle_of = lambda: lax.axis_index("row") * NEAR + lax.axis_index("near")
    first_of = lambda: lax.axis_index("far") * NEAR

    tilesum, shear, offset, across = pl.pallas_call(
        lambda *refs: sums(*refs, row_of=row_of, angle_of=angle_of, factor=factor),
        out_shape=(
            pltpu.VMEM((angles * slices, lanes), f32),
            pltpu.VMEM((NEAR,) + shear_weights.shape[1:], shear_weights.dtype),
            pltpu.VMEM((8, lanes), shear_offsets.dtype),
            pltpu.VMEM((slab_rows, 3 * angles), jnp.bfloat16),
        ),
        in_specs=[ANY, ANY, ANY, ANY],
        out_specs=(VMEM, VMEM, VMEM, VMEM),
        scratch_shapes=[
            pltpu.VMEM(volume.shape, f32),
            pltpu.VMEM(ray_weights.shape, f32),
            pltpu.VMEM(ray_weights.shape, f32),
            pltpu.SMEM(shear_offsets.shape, shear_offsets.dtype),
            pltpu.SemaphoreType.DMA((2,)),
            pltpu.SemaphoreType.DMA,
            pltpu.SemaphoreType.DMA,
            pltpu.SemaphoreType.DMA,
        ],
        name="sums",
    )(volume, ray_weights, shear_weights, shear_offsets)
    received = exchange(tilesum.reshape(angles, slices, lanes), ("row", "near"), peers)
    line = pl.pallas_call(
        lambda *refs: push(*refs, first_of=first_of),
        out_shape=tiles_of(cols),
        in_specs=[VMEM, VMEM],
        out_specs=VMEM,
        scratch_shapes=[tiles_of(2 * (cols + NEAR))],
        name="push",
    )(near(offset), near(received))
    parts = exchange(line, ("far", "near"))
    answer, residual = pl.pallas_call(
        lambda *refs: middle(*refs, factor=factor),
        out_shape=(tiles_of(cols), tiles_of(NEAR)),
        in_specs=[VMEM, VMEM, VMEM],
        out_specs=(VMEM, VMEM),
        name="middle",
    )(near(parts), near(shear), near(measured))
    returned = exchange(answer, ("far", "near"))
    tiles = pl.pallas_call(
        lambda *refs: pull(*refs, first_of=first_of),
        out_shape=tiles_of(angles),
        in_specs=[VMEM, VMEM],
        out_specs=VMEM,
        scratch_shapes=[tiles_of(cols + NEAR)],
        name="pull",
    )(near(offset), near(returned))
    arrived = exchange(tiles, ("row", "near"), peers).reshape(angles * slices, lanes)
    gradient, residual = pl.pallas_call(
        spread_back,
        out_shape=(jax.ShapeDtypeStruct(volume.shape, f32), jax.ShapeDtypeStruct(residual.shape, f32)),
        in_specs=[VMEM, VMEM, VMEM],
        out_specs=(ANY, ANY),
        scratch_shapes=[
            pltpu.VMEM(volume.shape, f32),
            pltpu.SemaphoreType.DMA((slices // 2,)),
            pltpu.SemaphoreType.DMA,
        ],
        name="spread_back",
    )(near(arrived), near(across), near(residual))
    return (residual, gradient)


def solution(mesh):
    rows, cols = mesh.devices.shape
    cut = Mesh(mesh.devices.reshape(rows, cols // NEAR, NEAR), ("row", "far", "near"))
    columns = ("far", "near")
    placed = (P(None, "row", columns), P(None, "row"), P(), P(), P("row", None, columns))
    return jax.shard_map(
        on_device,
        mesh=cut,
        in_specs=placed,
        out_specs=(P("row", None, columns), P(None, "row", columns)),
        check_vma=False,
    )
```

```python
import math

import jax
import jax.numpy as jnp
from jax import lax
from jax.experimental import pallas as pl
from jax.experimental.pallas import tpu as pltpu
from jax.sharding import Mesh, PartitionSpec as P

NEAR = 4
ANY = pl.BlockSpec(memory_space=pl.ANY)
VMEM = pl.BlockSpec(memory_space=pltpu.VMEM)


def row_order(rows):
    return sorted(range(rows), key=lambda r: (r % 2 == 0, -r))


def split(values):
    high = values.astype(jnp.bfloat16)
    return high, (values - high.astype(jnp.float32)).astype(jnp.bfloat16)


def dot(left, right, contract):
    return lax.dot_general(left, right, ((contract[:1], contract[1:]), ((), ())), preferred_element_type=jnp.float32)


def sums(volume_ref, weights_ref, shear_ref, offsets_ref, tiles_ref, owned_ref, offset_ref, across_ref, slab_ref, rays_ref, sorted_ref, table_ref, slab_sems, rays_sem, shear_sem, table_sem, *, row_of, angle_of, factor):
    slices, _, lanes = slab_ref.shape
    angles = rays_ref.shape[0]
    owned = owned_ref.shape[0]
    half = slices // 2
    rays_copy = pltpu.make_async_copy(weights_ref, rays_ref, rays_sem)
    slab_copies = [
        pltpu.make_async_copy(volume_ref.at[pl.ds(s, half)], slab_ref.at[pl.ds(s, half)], slab_sems.at[s // half])
        for s in range(0, slices, half)
    ]
    shear_copy = pltpu.make_async_copy(shear_ref.at[pl.ds(row_of() * owned, owned)], owned_ref, shear_sem)
    table_copy = pltpu.make_async_copy(offsets_ref, table_ref, table_sem)
    for copy in (rays_copy, *slab_copies, shear_copy, table_copy):
        copy.start()
    rays_copy.wait()
    for i, r in enumerate(row_order(angles // NEAR)):
        sorted_ref[i * NEAR : (i + 1) * NEAR, :] = rays_ref[r * NEAR : (r + 1) * NEAR, :]
    rays = sorted_ref[...]
    rays_high, rays_low = split(rays)
    rays_both = jnp.concatenate([rays_high, rays_low], axis=0)
    scaled = rays * factor
    high = scaled.astype(jnp.bfloat16).astype(jnp.float32)
    across_ref[...] = jnp.concatenate([high, high, scaled - high], axis=0).T.astype(jnp.bfloat16)
    for s in range(0, slices, half):
        slab_copies[s // half].wait()
        high, low = split(jnp.concatenate([slab_ref[s + t] for t in range(half)], axis=1))
        both = dot(rays_both, high, (1, 0))
        tiles = both[:angles] + both[angles:] + dot(rays_high, low, (1, 0))
        for t in range(half):
            tiles_ref[pl.ds(s + t, angles, stride=slices), :] = tiles[:, t * lanes : (t + 1) * lanes]
    table_copy.wait()
    offset_ref[...] = jnp.full(offset_ref.shape, table_ref[angle_of()], offset_ref.dtype)
    shear_copy.wait()


def push(offset_ref, tiles_ref, line_ref, sum_ref, *, first_of):
    cols = line_ref.shape[0]
    rows = tiles_ref.shape[0] // NEAR
    room = sum_ref.shape[0] // 2
    offset = offset_ref[0, 0]
    first = first_of()
    sum_ref[...] = jnp.zeros_like(sum_ref)
    for i, r in enumerate(row_order(rows)):
        window = pl.ds(lax.rem(first + offset * r, cols) + i % 2 * room, NEAR)
        sum_ref[window] = sum_ref[window] + tiles_ref[i * NEAR : (i + 1) * NEAR]
    for c in range(0, cols, NEAR):
        block = sum_ref[c : c + NEAR] + sum_ref[room + c : room + c + NEAR]
        if c == 0:
            block = block + (sum_ref[cols:room] + sum_ref[room + cols :])
        line_ref[cols - NEAR - c : cols - c] = block


def pull(offset_ref, line_ref, tiles_ref, twice_ref, *, first_of):
    cols = line_ref.shape[0]
    rows = tiles_ref.shape[0] // NEAR
    offset = offset_ref[0, 0]
    first = first_of()
    for c in range(0, cols, NEAR):
        twice_ref[c : c + NEAR] = line_ref[cols - NEAR - c : cols - c]
    twice_ref[cols:] = line_ref[cols - NEAR :]
    for i, r in enumerate(row_order(rows)):
        tiles_ref[i * NEAR : (i + 1) * NEAR] = twice_ref[pl.ds(lax.rem(first + offset * r, cols), NEAR)]


def middle(parts_ref, shear_ref, measured_ref, copies_ref, residual_ref, *, factor):
    count, slices, _ = parts_ref.shape
    residuals = []
    for j in range(NEAR):
        shares = [parts_ref[t] for t in range(j, count, NEAR)]
        while len(shares) > 1:
            shares = [sum(shares[t : t + 2]) for t in range(0, len(shares), 2)]
        both = dot(jnp.concatenate(split(shares[0] * factor), axis=0), shear_ref[j], (1, 0))
        residuals.append(both[:slices] + both[slices:] - measured_ref[j])
    for j in range(NEAR):
        residual_ref[j] = residuals[j]
        both = dot(jnp.concatenate(split(residuals[j]), axis=0), shear_ref[j], (1, 1))
        returning = both[:slices] + both[slices:]
        for t in range(j, count, NEAR):
            copies_ref[t] = returning


def spread_back(tiles_ref, across_ref, residual_ref, out_ref, residual_out_ref, slab_ref, sems, residual_sem):
    slices, _, lanes = slab_ref.shape
    angles = tiles_ref.shape[0] // slices
    residual_copy = pltpu.make_async_copy(residual_ref, residual_out_ref, residual_sem)
    residual_copy.start()
    across = across_ref[...]
    copies = []
    for s in range(0, slices, 2):
        pair = [tiles_ref[pl.ds(t, angles, stride=slices), :] for t in (s, s + 1)]
        high, low = split(jnp.concatenate(pair, axis=1))
        slab = dot(across, jnp.concatenate([high, low, high], axis=0), (1, 0))
        slab_ref[s] = slab[:, :lanes]
        slab_ref[s + 1] = slab[:, lanes:]
        copy = pltpu.make_async_copy(slab_ref.at[pl.ds(s, 2)], out_ref.at[pl.ds(s, 2)], sems.at[s // 2])
        copy.start()
        copies.append(copy)
    for copy in copies:
        copy.wait()
    residual_copy.wait()


def exchange(values, axes, groups=None):
    return lax.all_to_all(values, axes, 0, 0, tiled=True, axis_index_groups=groups)


def near(values):
    return pltpu.with_memory_space_constraint(values, pltpu.VMEM)


def on_device(volume, ray_weights, shear_weights, shear_offsets, measured):
    rows = lax.axis_size("row")
    cols = lax.axis_size(("far", "near"))
    slices, slab_rows, lanes = volume.shape
    angles = ray_weights.shape[0]
    factor = 1.0 / math.sqrt(slab_rows * rows)
    f32 = jnp.float32
    peers = [[r * NEAR + k for r in row_order(rows) for k in range(NEAR)]]
    columns = [[c + k for c in range(cols - NEAR, -1, -NEAR) for k in range(NEAR)]]
    tiles_of = lambda count: pltpu.VMEM((count, slices, lanes), f32)
    row_of = lambda: lax.axis_index("row")
    angle_of = lambda: lax.axis_index("row") * NEAR + lax.axis_index("near")
    first_of = lambda: lax.axis_index("far") * NEAR

    tilesum, shear, offset, across = pl.pallas_call(
        lambda *refs: sums(*refs, row_of=row_of, angle_of=angle_of, factor=factor),
        out_shape=(
            pltpu.VMEM((angles * slices, lanes), f32),
            pltpu.VMEM((NEAR,) + shear_weights.shape[1:], shear_weights.dtype),
            pltpu.VMEM((8, lanes), shear_offsets.dtype),
            pltpu.VMEM((slab_rows, 3 * angles), jnp.bfloat16),
        ),
        in_specs=[ANY, ANY, ANY, ANY],
        out_specs=(VMEM, VMEM, VMEM, VMEM),
        scratch_shapes=[
            pltpu.VMEM(volume.shape, f32),
            pltpu.VMEM(ray_weights.shape, f32),
            pltpu.VMEM(ray_weights.shape, f32),
            pltpu.SMEM(shear_offsets.shape, shear_offsets.dtype),
            pltpu.SemaphoreType.DMA((2,)),
            pltpu.SemaphoreType.DMA,
            pltpu.SemaphoreType.DMA,
            pltpu.SemaphoreType.DMA,
        ],
        name="sums",
    )(volume, ray_weights, shear_weights, shear_offsets)
    received = exchange(tilesum.reshape(angles, slices, lanes), ("row", "near"), peers)
    line = pl.pallas_call(
        lambda *refs: push(*refs, first_of=first_of),
        out_shape=tiles_of(cols),
        in_specs=[VMEM, VMEM],
        out_specs=VMEM,
        scratch_shapes=[tiles_of(2 * (cols + NEAR))],
        name="push",
    )(near(offset), near(received))
    parts = exchange(line, ("far", "near"), columns)
    answer, residual = pl.pallas_call(
        lambda *refs: middle(*refs, factor=factor),
        out_shape=(tiles_of(cols), tiles_of(NEAR)),
        in_specs=[VMEM, VMEM, VMEM],
        out_specs=(VMEM, VMEM),
        name="middle",
    )(near(parts), near(shear), near(measured))
    returned = exchange(answer, ("far", "near"), columns)
    tiles = pl.pallas_call(
        lambda *refs: pull(*refs, first_of=first_of),
        out_shape=tiles_of(angles),
        in_specs=[VMEM, VMEM],
        out_specs=VMEM,
        scratch_shapes=[tiles_of(cols + NEAR)],
        name="pull",
    )(near(offset), near(returned))
    arrived = exchange(tiles, ("row", "near"), peers).reshape(angles * slices, lanes)
    gradient, residual = pl.pallas_call(
        spread_back,
        out_shape=(jax.ShapeDtypeStruct(volume.shape, f32), jax.ShapeDtypeStruct(residual.shape, f32)),
        in_specs=[VMEM, VMEM, VMEM],
        out_specs=(ANY, ANY),
        scratch_shapes=[
            pltpu.VMEM(volume.shape, f32),
            pltpu.SemaphoreType.DMA((slices // 2,)),
            pltpu.SemaphoreType.DMA,
        ],
        name="spread_back",
    )(near(arrived), near(across), near(residual))
    return (residual, gradient)


def solution(mesh):
    rows, cols = mesh.devices.shape
    cut = Mesh(mesh.devices.reshape(rows, cols // NEAR, NEAR), ("row", "far", "near"))
    columns = ("far", "near")
    placed = (P(None, "row", columns), P(None, "row"), P(), P(), P("row", None, columns))
    return jax.shard_map(
        on_device,
        mesh=cut,
        in_specs=placed,
        out_specs=(P("row", None, columns), P(None, "row", columns)),
        check_vma=False,
    )
```

```python
import math

import jax
import jax.numpy as jnp
from jax import lax
from jax.experimental import pallas as pl
from jax.experimental.pallas import tpu as pltpu
from jax.sharding import Mesh, PartitionSpec as P

NEAR = 4
ANY = pl.BlockSpec(memory_space=pl.ANY)
VMEM = pl.BlockSpec(memory_space=pltpu.VMEM)


def row_order(rows):
    return sorted(range(rows), key=lambda r: (r % 2 == 0, -r))


def block_order(blocks):
    return sorted(range(blocks), key=lambda f: (-min(f, blocks - f), -f if f * 2 == blocks else f))


def split(values):
    high = values.astype(jnp.bfloat16)
    return high, (values - high.astype(jnp.float32)).astype(jnp.bfloat16)


def dot(left, right, contract):
    return lax.dot_general(left, right, ((contract[:1], contract[1:]), ((), ())), preferred_element_type=jnp.float32)


def sums(volume_ref, weights_ref, shear_ref, offsets_ref, tiles_ref, owned_ref, offset_ref, across_ref, slab_ref, rays_ref, sorted_ref, table_ref, slab_sems, rays_sem, shear_sem, table_sem, *, row_of, angle_of, factor):
    slices, _, lanes = slab_ref.shape
    angles = rays_ref.shape[0]
    owned = owned_ref.shape[0]
    half = slices // 2
    rays_copy = pltpu.make_async_copy(weights_ref, rays_ref, rays_sem)
    slab_copies = [
        pltpu.make_async_copy(volume_ref.at[pl.ds(s, half)], slab_ref.at[pl.ds(s, half)], slab_sems.at[s // half])
        for s in range(0, slices, half)
    ]
    shear_copy = pltpu.make_async_copy(shear_ref.at[pl.ds(row_of() * owned, owned)], owned_ref, shear_sem)
    table_copy = pltpu.make_async_copy(offsets_ref, table_ref, table_sem)
    for copy in (rays_copy, *slab_copies, shear_copy, table_copy):
        copy.start()
    rays_copy.wait()
    for i, r in enumerate(row_order(angles // NEAR)):
        sorted_ref[i * NEAR : (i + 1) * NEAR, :] = rays_ref[r * NEAR : (r + 1) * NEAR, :]
    rays = sorted_ref[...]
    rays_high, rays_low = split(rays)
    rays_both = jnp.concatenate([rays_high, rays_low], axis=0)
    scaled = rays * factor
    high = scaled.astype(jnp.bfloat16).astype(jnp.float32)
    across_ref[...] = jnp.concatenate([high, high, scaled - high], axis=0).T.astype(jnp.bfloat16)
    for s in range(0, slices, half):
        slab_copies[s // half].wait()
        high, low = split(jnp.concatenate([slab_ref[s + t] for t in range(half)], axis=1))
        both = dot(rays_both, high, (1, 0))
        tiles = both[:angles] + both[angles:] + dot(rays_high, low, (1, 0))
        for t in range(half):
            tiles_ref[pl.ds(s + t, angles, stride=slices), :] = tiles[:, t * lanes : (t + 1) * lanes]
    table_copy.wait()
    offset_ref[...] = jnp.full(offset_ref.shape, table_ref[angle_of()], offset_ref.dtype)
    shear_copy.wait()


def push(offset_ref, tiles_ref, line_ref, sum_ref, *, first_of):
    cols = line_ref.shape[0]
    rows = tiles_ref.shape[0] // NEAR
    room = sum_ref.shape[0] // 2
    offset = offset_ref[0, 0]
    first = first_of()
    sum_ref[...] = jnp.zeros_like(sum_ref)
    for i, r in enumerate(row_order(rows)):
        window = pl.ds(lax.rem(first + offset * r, cols) + i % 2 * room, NEAR)
        sum_ref[window] = sum_ref[window] + tiles_ref[i * NEAR : (i + 1) * NEAR]
    for i, f in enumerate(block_order(cols // NEAR)):
        c = f * NEAR
        block = sum_ref[c : c + NEAR] + sum_ref[room + c : room + c + NEAR]
        if c == 0:
            block = block + (sum_ref[cols:room] + sum_ref[room + cols :])
        line_ref[i * NEAR : (i + 1) * NEAR] = block


def pull(offset_ref, line_ref, tiles_ref, twice_ref, *, first_of):
    cols = line_ref.shape[0]
    rows = tiles_ref.shape[0] // NEAR
    offset = offset_ref[0, 0]
    first = first_of()
    for i, f in enumerate(block_order(cols // NEAR)):
        twice_ref[f * NEAR : (f + 1) * NEAR] = line_ref[i * NEAR : (i + 1) * NEAR]
    twice_ref[cols:] = twice_ref[:NEAR]
    for i, r in enumerate(row_order(rows)):
        tiles_ref[i * NEAR : (i + 1) * NEAR] = twice_ref[pl.ds(lax.rem(first + offset * r, cols), NEAR)]


def middle(parts_ref, shear_ref, measured_ref, copies_ref, residual_ref, *, factor):
    count, slices, _ = parts_ref.shape
    residuals = []
    for j in range(NEAR):
        shares = [parts_ref[t] for t in range(j, count, NEAR)]
        while len(shares) > 1:
            shares = [sum(shares[t : t + 2]) for t in range(0, len(shares), 2)]
        both = dot(jnp.concatenate(split(shares[0] * factor), axis=0), shear_ref[j], (1, 0))
        residuals.append(both[:slices] + both[slices:] - measured_ref[j])
    for j in range(NEAR):
        residual_ref[j] = residuals[j]
        both = dot(jnp.concatenate(split(residuals[j]), axis=0), shear_ref[j], (1, 1))
        returning = both[:slices] + both[slices:]
        for t in range(j, count, NEAR):
            copies_ref[t] = returning


def spread_back(tiles_ref, across_ref, residual_ref, out_ref, residual_out_ref, slab_ref, sems, residual_sem):
    slices, _, lanes = slab_ref.shape
    angles = tiles_ref.shape[0] // slices
    residual_copy = pltpu.make_async_copy(residual_ref, residual_out_ref, residual_sem)
    residual_copy.start()
    across = across_ref[...]
    copies = []
    for s in range(0, slices, 2):
        pair = [tiles_ref[pl.ds(t, angles, stride=slices), :] for t in (s, s + 1)]
        high, low = split(jnp.concatenate(pair, axis=1))
        slab = dot(across, jnp.concatenate([high, low, high], axis=0), (1, 0))
        slab_ref[s] = slab[:, :lanes]
        slab_ref[s + 1] = slab[:, lanes:]
        copy = pltpu.make_async_copy(slab_ref.at[pl.ds(s, 2)], out_ref.at[pl.ds(s, 2)], sems.at[s // 2])
        copy.start()
        copies.append(copy)
    for copy in copies:
        copy.wait()
    residual_copy.wait()


def exchange(values, axes, groups=None):
    return lax.all_to_all(values, axes, 0, 0, tiled=True, axis_index_groups=groups)


def near(values):
    return pltpu.with_memory_space_constraint(values, pltpu.VMEM)


def on_device(volume, ray_weights, shear_weights, shear_offsets, measured):
    rows = lax.axis_size("row")
    cols = lax.axis_size(("far", "near"))
    slices, slab_rows, lanes = volume.shape
    angles = ray_weights.shape[0]
    factor = 1.0 / math.sqrt(slab_rows * rows)
    f32 = jnp.float32
    peers = [[r * NEAR + k for r in row_order(rows) for k in range(NEAR)]]
    columns = [[f * NEAR + k for f in block_order(cols // NEAR) for k in range(NEAR)]]
    tiles_of = lambda count: pltpu.VMEM((count, slices, lanes), f32)
    row_of = lambda: lax.axis_index("row")
    angle_of = lambda: lax.axis_index("row") * NEAR + lax.axis_index("near")
    first_of = lambda: lax.axis_index("far") * NEAR

    tilesum, shear, offset, across = pl.pallas_call(
        lambda *refs: sums(*refs, row_of=row_of, angle_of=angle_of, factor=factor),
        out_shape=(
            pltpu.VMEM((angles * slices, lanes), f32),
            pltpu.VMEM((NEAR,) + shear_weights.shape[1:], shear_weights.dtype),
            pltpu.VMEM((8, lanes), shear_offsets.dtype),
            pltpu.VMEM((slab_rows, 3 * angles), jnp.bfloat16),
        ),
        in_specs=[ANY, ANY, ANY, ANY],
        out_specs=(VMEM, VMEM, VMEM, VMEM),
        scratch_shapes=[
            pltpu.VMEM(volume.shape, f32),
            pltpu.VMEM(ray_weights.shape, f32),
            pltpu.VMEM(ray_weights.shape, f32),
            pltpu.SMEM(shear_offsets.shape, shear_offsets.dtype),
            pltpu.SemaphoreType.DMA((2,)),
            pltpu.SemaphoreType.DMA,
            pltpu.SemaphoreType.DMA,
            pltpu.SemaphoreType.DMA,
        ],
        name="sums",
    )(volume, ray_weights, shear_weights, shear_offsets)
    received = exchange(tilesum.reshape(angles, slices, lanes), ("row", "near"), peers)
    line = pl.pallas_call(
        lambda *refs: push(*refs, first_of=first_of),
        out_shape=tiles_of(cols),
        in_specs=[VMEM, VMEM],
        out_specs=VMEM,
        scratch_shapes=[tiles_of(2 * (cols + NEAR))],
        name="push",
    )(near(offset), near(received))
    parts = exchange(line, ("far", "near"), columns)
    answer, residual = pl.pallas_call(
        lambda *refs: middle(*refs, factor=factor),
        out_shape=(tiles_of(cols), tiles_of(NEAR)),
        in_specs=[VMEM, VMEM, VMEM],
        out_specs=(VMEM, VMEM),
        name="middle",
    )(near(parts), near(shear), near(measured))
    returned = exchange(answer, ("far", "near"), columns)
    tiles = pl.pallas_call(
        lambda *refs: pull(*refs, first_of=first_of),
        out_shape=tiles_of(angles),
        in_specs=[VMEM, VMEM],
        out_specs=VMEM,
        scratch_shapes=[tiles_of(cols + NEAR)],
        name="pull",
    )(near(offset), near(returned))
    arrived = exchange(tiles, ("row", "near"), peers).reshape(angles * slices, lanes)
    gradient, residual = pl.pallas_call(
        spread_back,
        out_shape=(jax.ShapeDtypeStruct(volume.shape, f32), jax.ShapeDtypeStruct(residual.shape, f32)),
        in_specs=[VMEM, VMEM, VMEM],
        out_specs=(ANY, ANY),
        scratch_shapes=[
            pltpu.VMEM(volume.shape, f32),
            pltpu.SemaphoreType.DMA((slices // 2,)),
            pltpu.SemaphoreType.DMA,
        ],
        name="spread_back",
    )(near(arrived), near(across), near(residual))
    return (residual, gradient)


def solution(mesh):
    rows, cols = mesh.devices.shape
    cut = Mesh(mesh.devices.reshape(rows, cols // NEAR, NEAR), ("row", "far", "near"))
    columns = ("far", "near")
    placed = (P(None, "row", columns), P(None, "row"), P(), P(), P("row", None, columns))
    return jax.shard_map(
        on_device,
        mesh=cut,
        in_specs=placed,
        out_specs=(P("row", None, columns), P(None, "row", columns)),
        check_vma=False,
    )
```
